32 devices in a mesh: tm: 8 (over y, x, core), space: 4 (over z).
Axes of the slice: x: 2, y: 2, z: 4, core: 2. Of those that a mesh axis runs over, the one named last changes fastest.
Arguments:
- hits: int32 [64, 128, 256], P('tm', 'space'), may hold values from 0 to 12
- misses: int32 [64, 128, 256], P('tm', 'space'), may hold values from 0 to 12
Outputs:
- occupancy: float32 [64, 128, 256], P('tm', 'space')
- spread: float32 [64, 128, 256], P('tm', 'space')
The draws below stay inside these ranges and needn't reach their ends.
All inputs are finite; a program needn't handle non-finite values.
Results may differ from the reference program's by a relative error of at most 0.00019.
Values sent between devices are 32-bit elements; how exact they have to be, the bound alone decides.
A program may use at most 64 MiB of HBM per device.

```python
import math
import jax
import jax.numpy as jnp
from jax import lax

COLS = 256
RADIUS = 7
SCALE_T = 64
FRAMES = 64
ROWS = 128


def count_caps(key):
    base_key = jax.random.fold_in(key, 17)
    keys = jax.random.split(base_key, 8)
    shape = (FRAMES, ROWS, COLS)
    frame_index = lax.broadcasted_iota(jnp.int32, shape, 0)
    row_index = lax.broadcasted_iota(jnp.int32, shape, 1)
    column_index = lax.broadcasted_iota(jnp.int32, shape, 2)
    blob_count = 6
    centre_row = jax.random.randint(keys[0], (blob_count,), 0, ROWS, dtype=jnp.int32)
    centre_column = jax.random.randint(keys[1], (blob_count,), 0, COLS, dtype=jnp.int32)
    speed_row = jax.random.randint(keys[2], (blob_count,), -3, 4, dtype=jnp.int32)
    speed_column = jax.random.randint(keys[3], (blob_count,), -3, 4, dtype=jnp.int32)
    half_row = max(ROWS // 6, 3)
    half_column = max(COLS // 6, 3)
    inside = jnp.zeros(shape, jnp.bool_)
    for blob in range(blob_count):
        place_row = jnp.mod(centre_row[blob] + jnp.floor_divide(speed_row[blob] * frame_index, 3), ROWS)
        place_column = jnp.mod(centre_column[blob] + jnp.floor_divide(speed_column[blob] * frame_index, 3), COLS)
        gap_row = jnp.mod(row_index - place_row, ROWS)
        gap_row = jnp.minimum(gap_row, ROWS - gap_row)
        gap_column = jnp.mod(column_index - place_column, COLS)
        gap_column = jnp.minimum(gap_column, COLS - gap_column)
        inside = jnp.logical_or(inside, gap_row * half_column + gap_column * half_row <= half_row * half_column)
    window_count = 4
    start_frame = jax.random.randint(keys[4], (window_count,), 0, FRAMES, dtype=jnp.int32)
    start_row = jax.random.randint(keys[5], (window_count,), 0, ROWS, dtype=jnp.int32)
    start_column = jax.random.randint(keys[6], (window_count,), 0, COLS, dtype=jnp.int32)
    span_frame = max(FRAMES // 3, 1)
    span_row = max(ROWS // 3, 1)
    span_column = max(COLS // 3, 1)
    blind = jnp.zeros(shape, jnp.bool_)
    for window in range(window_count):
        in_time = jnp.mod(frame_index - start_frame[window], FRAMES) < span_frame
        in_rows = jnp.mod(row_index - start_row[window], ROWS) < span_row
        in_columns = jnp.mod(column_index - start_column[window], COLS) < span_column
        blind = jnp.logical_or(blind, jnp.logical_and(in_time, jnp.logical_and(in_rows, in_columns)))
    level = 1 + jnp.floor_divide(row_index * 4, ROWS)
    hit_cap = jnp.where(inside, 12, level - 1)
    miss_cap = jnp.where(inside, level - 1, 12)
    hit_cap = jnp.where(blind, 0, hit_cap).astype(jnp.int32)
    miss_cap = jnp.where(blind, 0, miss_cap).astype(jnp.int32)
    return (hit_cap, miss_cap, keys[7])


def draw_hits(key, part):
    hit_cap, miss_cap, count_key = count_caps(key)
    return jax.random.randint(jax.random.fold_in(count_key, 1), (FRAMES, ROWS, COLS), 0, hit_cap + 1, dtype=jnp.int32)


def draw_misses(key, part):
    hit_cap, miss_cap, count_key = count_caps(key)
    return jax.random.randint(jax.random.fold_in(count_key, 2), (FRAMES, ROWS, COLS), 0, miss_cap + 1, dtype=jnp.int32)


def setup_inputs(seed: int = 0) -> dict:
    streams_of = jax.random.split(jax.random.key(seed), 3)
    hits = draw_hits(jax.random.fold_in(streams_of[2], 71), 0)
    misses = draw_misses(jax.random.fold_in(streams_of[2], 71), 0)
    return dict(hits=hits, misses=misses)


sigma_cells = 3.0
prior_var = 4.0

def mat_mul(a, b):
    return (a[0] * b[0] + a[1] * b[2], a[0] * b[1] + a[1] * b[3], a[2] * b[0] + a[3] * b[2], a[2] * b[1] + a[3] * b[3])

def mat_add(a, b):
    return tuple((x + y for x, y in zip(a, b)))

def mat_sub(a, b):
    return tuple((x - y for x, y in zip(a, b)))

def transpose(a):
    return (a[0], a[2], a[1], a[3])

def as_full(s):
    return (s[0], s[1], s[1], s[2])

def as_sym(a):
    return (a[0], 0.5 * (a[1] + a[2]), a[3])

def mat_vec(a, v):
    return (a[0] * v[0] + a[1] * v[1], a[2] * v[0] + a[3] * v[1])

def vec_add(u, v):
    return (u[0] + v[0], u[1] + v[1])

def vec_sub(u, v):
    return (u[0] - v[0], u[1] - v[1])

def inverse(a):
    determ = a[0] * a[3] - a[1] * a[2]
    return (a[3] / determ, -a[1] / determ, -a[2] / determ, a[0] / determ)

def dynamics():
    decay_rate = math.sqrt(3.0) / SCALE_T
    factor = math.exp(-decay_rate)
    transit = (factor * (1.0 + decay_rate), factor, -factor * decay_rate * decay_rate, factor * (1.0 - decay_rate))
    prior_p = (prior_var, 0.0, prior_var * decay_rate * decay_rate)
    carried = mat_mul(mat_mul(transit, as_full(prior_p)), transpose(transit))
    noise_q = (prior_p[0] - carried[0], prior_p[1] - 0.5 * (carried[1] + carried[2]), prior_p[2] - carried[3])
    return (transit, prior_p, noise_q)

def kernel_taps():
    offsets = jnp.arange(-RADIUS, RADIUS + 1).astype(jnp.float32)
    weights = jnp.exp(-offsets * offsets / (2.0 * sigma_cells * sigma_cells))
    return weights / jnp.sum(weights)

def band_matrix(col_count):
    offsets = jnp.arange(-RADIUS, RADIUS + 1).astype(jnp.float32)
    total = jnp.sum(jnp.exp(-offsets * offsets / (2.0 * sigma_cells * sigma_cells)))
    index = jnp.arange(col_count)
    offset = (index[:, None] - index[None, :]).astype(jnp.float32)
    weights = jnp.exp(-offset * offset / (2.0 * sigma_cells * sigma_cells)) / total
    return jnp.where(jnp.abs(offset) <= RADIUS, weights, jnp.zeros_like(weights))

def reference(hits, misses):
    count_total = (hits + misses).astype(jnp.float32)
    hit_plus = hits.astype(jnp.float32) + 1.0
    miss_plus = misses.astype(jnp.float32) + 1.0
    both_plus = hit_plus + miss_plus
    weight = count_total * hit_plus * miss_plus / (both_plus * both_plus)
    logit = jnp.log(hit_plus / miss_plus)
    channels = jnp.stack([weight * logit, weight])
    row_count = channels.shape[2]
    col_count = channels.shape[3]
    padded = jnp.pad(channels, ((0, 0), (0, 0), (RADIUS, RADIUS), (0, 0)))
    taps_row = kernel_taps()
    rowsum = jnp.zeros_like(channels)
    for shift_row in range(2 * RADIUS + 1):
        rowsum = rowsum + taps_row[shift_row] * padded[:, :, shift_row:shift_row + row_count, :]
    colsum = jnp.dot(rowsum.reshape(-1, col_count), band_matrix(col_count), precision=lax.Precision.HIGHEST, preferred_element_type=jnp.float32).reshape(channels.shape)
    numerator = colsum[0]
    denominator = colsum[1]
    transit, prior_p, noise_q = dynamics()
    zeros_cell = jnp.zeros(numerator.shape[1:], jnp.float32)
    start = (zeros_cell, zeros_cell, zeros_cell + prior_p[0], zeros_cell + prior_p[1], zeros_cell + prior_p[2])

    def advance(state_in, frame_data):
        num_val, den_val = frame_data
        mean_a, mean_b, cov_aa, cov_ab, cov_bb = state_in
        scale_s = 1.0 + cov_aa * den_val
        moved = (num_val - den_val * mean_a) / scale_s
        gain_a = cov_aa * den_val / scale_s
        gain_b = cov_ab * den_val / scale_s
        filt = (mean_a + cov_aa * moved, mean_b + cov_ab * moved, cov_aa - gain_a * cov_aa, cov_ab - gain_a * cov_ab, cov_bb - gain_b * cov_ab)
        pred_mean = mat_vec(transit, filt[:2])
        pred_cov = as_sym(mat_add(mat_mul(mat_mul(transit, as_full(filt[2:])), transpose(transit)), as_full(noise_q)))
        return (pred_mean + pred_cov, filt)
    ignored, filtered = lax.scan(advance, start, (numerator, denominator))

    def retreat(state_in, filt_frame):
        later_mean = state_in[:2]
        later_cov = state_in[2:]
        mean_two = filt_frame[:2]
        cov = as_full(filt_frame[2:])
        predicted = mat_add(mat_mul(mat_mul(transit, cov), transpose(transit)), as_full(noise_q))
        gain_mat = mat_mul(mat_mul(cov, transpose(transit)), inverse(predicted))
        spread_gap = mat_sub(as_full(later_cov), predicted)
        new_cov = as_sym(mat_add(cov, mat_mul(mat_mul(gain_mat, spread_gap), transpose(gain_mat))))
        new_mean = vec_add(mean_two, mat_vec(gain_mat, vec_sub(later_mean, mat_vec(transit, mean_two))))
        result = new_mean + new_cov
        return (result, result)
    last_state = tuple((part[-1] for part in filtered))
    head_states = tuple((part[:-1] for part in filtered))
    ignored_two, smoothed = lax.scan(retreat, last_state, head_states, reverse=True)
    mean_value = jnp.concatenate([smoothed[0], last_state[0][None]], axis=0)
    var_value = jnp.concatenate([smoothed[2], last_state[2][None]], axis=0)
    return (jax.nn.sigmoid(mean_value), var_value)
```

```python
import functools
import math

import jax
import jax.numpy as jnp
from jax import lax
from jax.experimental import pallas as pl
from jax.experimental.pallas import tpu as pltpu
from jax.sharding import PartitionSpec as P

RADIUS = 7
SCALE_T = 64
SUB = 8
LANES = 128
SAVED = 7

sigma_cells = 3.0
prior_var = 4.0


def dynamics():
    rate = math.sqrt(3.0) / SCALE_T
    factor = math.exp(-rate)
    a, b, c, d = (
        factor * (1.0 + rate),
        factor,
        -factor * rate * rate,
        factor * (1.0 - rate),
    )
    p0, p1 = prior_var, prior_var * rate * rate
    noise = (
        p0 - (a * a * p0 + b * b * p1),
        -(a * c * p0 + b * d * p1),
        p1 - (c * c * p0 + d * d * p1),
    )
    return (a, b, c, d), (p0, p1), noise


def taps():
    raw = [math.exp(-o * o / (2.0 * sigma_cells**2)) for o in range(-RADIUS, RADIUS + 1)]
    total = sum(raw)
    return [r / total for r in raw], total


def kernel(tm_count, space_count, hits, misses, occ, spr, chan, horiz, window, send, recv, saved,
           back, landed, halo_send, halo_recv, go_send, go_recv, ret_send, ret_recv):
    frames, rows, cols = hits.shape
    halves = cols // LANES
    chunks = (rows // SUB) * halves
    stride = tm_count // chunks
    me = lax.axis_index("tm")
    tile = lax.axis_index("space")
    mine = me // stride
    (ta, tb, tc, td), (prior0, prior1), (q00, q01, q11) = dynamics()
    weights, total = taps()
    has_up = tile > 0
    has_down = tile < space_count - 1
    barrier = pltpu.get_barrier_semaphore()

    def greet(k, carry):
        pl.semaphore_signal(barrier, inc=1, device_id={"tm": (me + k) % tm_count})
        return carry

    lax.fori_loop(1, tm_count, greet, 0)

    @pl.when(has_up)
    def _():
        pl.semaphore_signal(barrier, inc=1, device_id={"space": tile - 1})

    @pl.when(has_down)
    def _():
        pl.semaphore_signal(barrier, inc=1, device_id={"space": tile + 1})

    own = pl.ds(SUB, rows)

    def observe(f, carry):
        h, m = hits[f], misses[f]
        hp = h.astype(jnp.float32) + 1.0
        mp = m.astype(jnp.float32) + 1.0
        both = hp + mp
        weight = (h + m).astype(jnp.float32) * hp * mp / (both * both)
        chan[0, f, own, :] = weight * jnp.log(hp / mp)
        chan[1, f, own, :] = weight
        return carry

    lax.fori_loop(0, frames, observe, 0)

    @pl.when(jnp.logical_not(has_up))
    def _():
        chan[:, :, 0:SUB, :] = jnp.zeros((2, frames, SUB, cols), jnp.float32)

    @pl.when(jnp.logical_not(has_down))
    def _():
        chan[:, :, SUB + rows :, :] = jnp.zeros((2, frames, SUB, cols), jnp.float32)

    neighbours = has_up.astype(jnp.int32) + has_down.astype(jnp.int32)
    pl.semaphore_wait(barrier, tm_count - 1 + neighbours)

    to_down = pltpu.make_async_remote_copy(
        src_ref=chan.at[:, :, pl.ds(rows, SUB), :],
        dst_ref=chan.at[:, :, pl.ds(0, SUB), :],
        send_sem=halo_send.at[0], recv_sem=halo_recv.at[0],
        device_id={"space": tile + 1})
    to_up = pltpu.make_async_remote_copy(
        src_ref=chan.at[:, :, pl.ds(SUB, SUB), :],
        dst_ref=chan.at[:, :, pl.ds(SUB + rows, SUB), :],
        send_sem=halo_send.at[1], recv_sem=halo_recv.at[1],
        device_id={"space": tile - 1})

    @pl.when(has_down)
    def _():
        to_down.start()

    @pl.when(has_up)
    def _():
        to_up.start()

    offset = (lax.broadcasted_iota(jnp.int32, (cols, cols), 0)
              - lax.broadcasted_iota(jnp.int32, (cols, cols), 1))
    far = offset.astype(jnp.float32)
    band = jnp.where(jnp.abs(offset) <= RADIUS,
                     jnp.exp(-far * far / (2.0 * sigma_cells**2)) / total, 0.0)

    def across(start, size):
        flat = chan[:, :, start : start + size, :].reshape(2 * frames * size, cols)
        out = jnp.dot(flat, band, precision=lax.Precision.HIGHEST,
                      preferred_element_type=jnp.float32)
        horiz[:, :, start : start + size, :] = out.reshape(2, frames, size, cols)

    across(SUB, rows)

    @pl.when(has_up)
    def _():
        to_down.wait_recv()

    @pl.when(has_down)
    def _():
        to_up.wait_recv()

    across(0, SUB)
    across(SUB + rows, SUB)

    def down_chunk(j):
        row0 = pl.multiple_of((j // halves) * SUB, SUB)
        col0 = pl.multiple_of((j % halves) * LANES, LANES)
        window[...] = horiz[:, :, pl.ds(row0, 3 * SUB), pl.ds(col0, LANES)]

        def at(s):
            first = SUB - RADIUS + s
            return window[:, :, first : first + SUB, :]

        out = weights[RADIUS] * at(RADIUS)
        for s in range(RADIUS):
            out = out + weights[s] * (at(s) + at(2 * RADIUS - s))
        return out

    def go_copy(j):
        return pltpu.make_async_remote_copy(
            src_ref=send.at[j], dst_ref=recv.at[me], send_sem=go_send.at[j],
            recv_sem=go_recv.at[me], device_id={"tm": j * stride})

    def scatter(k, carry):
        j = (mine + k) % chunks
        send[j] = down_chunk(j)
        go_copy(j).start()
        return carry

    lax.fori_loop(1, chunks, scatter, 0)
    if stride == 1:
        recv[me] = down_chunk(mine)
    else:
        send[mine] = down_chunk(mine)

        @pl.when(me % stride == 0)
        def _():
            recv[me] = send[mine]

        @pl.when(me % stride != 0)
        def _():
            go_copy(mine).start()

    def back_copy(i):
        return pltpu.make_async_remote_copy(
            src_ref=back.at[i], dst_ref=landed.at[mine], send_sem=ret_send.at[i],
            recv_sem=ret_recv.at[mine], device_id={"tm": i})

    def smooth():
        def forward(i, state):
            @pl.when(i != me)
            def _():
                pltpu.make_async_remote_copy(
                    src_ref=send.at[0], dst_ref=recv.at[i], send_sem=go_send.at[0],
                    recv_sem=go_recv.at[i], device_id={"tm": i}).wait_recv()

            m0, m1, p00, p01, p11 = state
            for f in range(frames):
                num, den = recv[i, 0, f], recv[i, 1, f]
                inv = 1.0 / (1.0 + p00 * den)
                w = den * inv
                e = (num - den * m0) * inv
                k1 = p01 * w
                m0, m1 = m0 + p00 * e, m1 + p01 * e
                p11 = p11 - k1 * p01
                p00, p01 = p00 * inv, p01 * inv
                for slot, value in enumerate((inv, w, e, k1, m0, p00, p01)):
                    saved[i, f, slot] = value
                m0, m1 = ta * m0 + tb * m1, tc * m0 + td * m1
                p00, p01, p11 = (
                    (ta * ta) * p00 + (2.0 * ta * tb) * p01 + ((tb * tb) * p11 + q00),
                    (ta * tc) * p00 + (ta * td + tb * tc) * p01 + ((tb * td) * p11 + q01),
                    (tc * tc) * p00 + (2.0 * tc * td) * p01 + ((td * td) * p11 + q11),
                )
            return m0, m1, p00, p01, p11

        zero = jnp.zeros((SUB, LANES), jnp.float32)
        lax.fori_loop(0, tm_count, forward, (zero, zero, zero + prior0, zero, zero + prior1))

        def backward(n, state):
            i = tm_count - 1 - n
            u0, u1, n00, n01, n11 = state
            for f in reversed(range(frames)):
                inv, w, e, k1, m0, p00, p01 = (saved[i, f, slot] for slot in range(SAVED))
                mean = m0 + p00 * u0 + p01 * u1
                back[i, 0, f] = 1.0 / (1.0 + jnp.exp(-mean))
                back[i, 1, f] = p00 - (
                    p00 * p00 * n00 + 2.0 * (p00 * p01) * n01 + p01 * p01 * n11)
                r0 = e + inv * u0 - k1 * u1
                l00 = w + (inv * inv) * n00 - (2.0 * inv * k1) * n01 + (k1 * k1) * n11
                l01 = inv * n01 - k1 * n11
                u0, u1 = ta * r0 + tc * u1, tb * r0 + td * u1
                n00, n01, n11 = (
                    (ta * ta) * l00 + ((2.0 * ta * tc) * l01 + (tc * tc) * n11),
                    (ta * tb) * l00 + ((ta * td + tb * tc) * l01 + (tc * td) * n11),
                    (tb * tb) * l00 + ((2.0 * tb * td) * l01 + (td * td) * n11),
                )

            @pl.when(i != me)
            def _():
                back_copy(i).start()

            @pl.when(i == me)
            def _():
                landed[mine] = back[i]

            return u0, u1, n00, n01, n11

        lax.fori_loop(0, tm_count, backward, (zero,) * 5)

    if stride == 1:
        smooth()
    else:
        pl.when(me % stride == 0)(smooth)

    def place(k, carry):
        j = (mine + k) % chunks

        @pl.when(j * stride != me)
        def _():
            pltpu.make_async_remote_copy(
                src_ref=back.at[0], dst_ref=landed.at[j], send_sem=ret_send.at[0],
                recv_sem=ret_recv.at[j], device_id={"tm": j * stride}).wait_recv()

        row0 = pl.multiple_of((j // halves) * SUB, SUB)
        col0 = pl.multiple_of((j % halves) * LANES, LANES)
        occ[:, pl.ds(row0, SUB), pl.ds(col0, LANES)] = landed[j, 0]
        spr[:, pl.ds(row0, SUB), pl.ds(col0, LANES)] = landed[j, 1]
        return carry

    lax.fori_loop(0, chunks, place, 0)

    @pl.when(has_down)
    def _():
        to_down.wait_send()

    @pl.when(has_up)
    def _():
        to_up.wait_send()

    def sent(j, carry):
        @pl.when(j * stride != me)
        def _():
            go_copy(j).wait_send()

        return carry

    lax.fori_loop(0, chunks, sent, 0)

    def returned(i, carry):
        @pl.when(jnp.logical_and(i != me, me % stride == 0))
        def _():
            back_copy(i).wait_send()

        return carry

    lax.fori_loop(0, tm_count, returned, 0)


def solution(mesh):
    tm_count, space_count = mesh.shape["tm"], mesh.shape["space"]

    def body(hits, misses):
        frames, rows, cols = hits.shape
        chunks = (rows // SUB) * (cols // LANES)
        cells = (SUB, LANES)
        vmem = pl.BlockSpec(memory_space=pltpu.VMEM)
        out = jax.ShapeDtypeStruct(hits.shape, jnp.float32)
        return pl.pallas_call(
            functools.partial(kernel, tm_count, space_count),
            out_shape=(out, out),
            in_specs=[vmem, vmem],
            out_specs=(vmem, vmem),
            scratch_shapes=[
                pltpu.VMEM((2, frames, rows + 2 * SUB, cols), jnp.float32),
                pltpu.VMEM((2, frames, rows + 2 * SUB, cols), jnp.float32),
                pltpu.VMEM((2, frames, 3 * SUB, LANES), jnp.float32),
                pltpu.VMEM((chunks, 2, frames) + cells, jnp.float32),
                pltpu.VMEM((tm_count, 2, frames) + cells, jnp.float32),
                pltpu.VMEM((tm_count, frames, SAVED) + cells, jnp.float32),
                pltpu.VMEM((tm_count, 2, frames) + cells, jnp.float32),
                pltpu.VMEM((chunks, 2, frames) + cells, jnp.float32),
                pltpu.SemaphoreType.DMA((2,)),
                pltpu.SemaphoreType.DMA((2,)),
                pltpu.SemaphoreType.DMA((chunks,)),
                pltpu.SemaphoreType.DMA((tm_count,)),
                pltpu.SemaphoreType.DMA((tm_count,)),
                pltpu.SemaphoreType.DMA((chunks,)),
            ],
            compiler_params=pltpu.CompilerParams(
                collective_id=0, has_side_effects=True, vmem_limit_bytes=48 * 1024 * 1024),
        )(hits, misses)

    placed = P("tm", "space", None)
    return jax.shard_map(body, mesh=mesh, in_specs=(placed, placed),
                         out_specs=(placed, placed), check_vma=False)
```

```python
import functools
import math

import jax
import jax.numpy as jnp
from jax import lax
from jax.experimental import pallas as pl
from jax.experimental.pallas import tpu as pltpu
from jax.sharding import PartitionSpec as P

RADIUS = 7
SCALE_T = 64
SUB = 8
LANES = 128
SAVED = 7

sigma_cells = 3.0
prior_var = 4.0


def dynamics():
    rate = math.sqrt(3.0) / SCALE_T
    factor = math.exp(-rate)
    a, b, c, d = (
        factor * (1.0 + rate),
        factor,
        -factor * rate * rate,
        factor * (1.0 - rate),
    )
    p0, p1 = prior_var, prior_var * rate * rate
    noise = (
        p0 - (a * a * p0 + b * b * p1),
        -(a * c * p0 + b * d * p1),
        p1 - (c * c * p0 + d * d * p1),
    )
    return (a, b, c, d), (p0, p1), noise


def taps():
    raw = [math.exp(-o * o / (2.0 * sigma_cells**2)) for o in range(-RADIUS, RADIUS + 1)]
    total = sum(raw)
    return [r / total for r in raw], total


def kernel(tm_count, space_count, hits_hbm, misses_hbm, occ, spr, hits, misses, chan, horiz, window, send, recv, saved,
           back, landed, halo_send, halo_recv, go_send, go_recv, ret_send, ret_recv, load):
    load_hits = pltpu.make_async_copy(hits_hbm, hits, load.at[0])
    load_misses = pltpu.make_async_copy(misses_hbm, misses, load.at[1])
    load_hits.start()
    load_misses.start()
    frames, rows, cols = hits.shape
    groups = rows // SUB
    halves = cols // LANES
    chunks = (rows // SUB) * halves
    stride = tm_count // chunks
    me = lax.axis_index("tm")
    tile = lax.axis_index("space")
    mine = me // stride
    (ta, tb, tc, td), (prior0, prior1), (q00, q01, q11) = dynamics()
    weights, total = taps()
    has_up = tile > 0
    has_down = tile < space_count - 1
    barrier = pltpu.get_barrier_semaphore()

    def greet(k, carry):
        pl.semaphore_signal(barrier, inc=1, device_id={"tm": (me + k) % tm_count})
        return carry

    lax.fori_loop(1, tm_count, greet, 0)

    @pl.when(has_up)
    def _():
        pl.semaphore_signal(barrier, inc=1, device_id={"space": tile - 1})

    @pl.when(has_down)
    def _():
        pl.semaphore_signal(barrier, inc=1, device_id={"space": tile + 1})

    own = pl.ds(SUB, rows)
    load_hits.wait()
    load_misses.wait()

    def observe(f, carry):
        h, m = hits[f], misses[f]
        hp = h.astype(jnp.float32) + 1.0
        mp = m.astype(jnp.float32) + 1.0
        both = hp + mp
        weight = (h + m).astype(jnp.float32) * hp * mp / (both * both)
        chan[0, f, own, :] = weight * jnp.log(hp / mp)
        chan[1, f, own, :] = weight
        return carry

    lax.fori_loop(0, frames, observe, 0)

    @pl.when(jnp.logical_not(has_up))
    def _():
        chan[:, :, 0:SUB, :] = jnp.zeros((2, frames, SUB, cols), jnp.float32)

    @pl.when(jnp.logical_not(has_down))
    def _():
        chan[:, :, SUB + rows :, :] = jnp.zeros((2, frames, SUB, cols), jnp.float32)

    neighbours = has_up.astype(jnp.int32) + has_down.astype(jnp.int32)
    pl.semaphore_wait(barrier, tm_count - 1 + neighbours)

    to_down = pltpu.make_async_remote_copy(
        src_ref=chan.at[:, :, pl.ds(rows, SUB), :],
        dst_ref=chan.at[:, :, pl.ds(0, SUB), :],
        send_sem=halo_send.at[0], recv_sem=halo_recv.at[0],
        device_id={"space": tile + 1})
    to_up = pltpu.make_async_remote_copy(
        src_ref=chan.at[:, :, pl.ds(SUB, SUB), :],
        dst_ref=chan.at[:, :, pl.ds(SUB + rows, SUB), :],
        send_sem=halo_send.at[1], recv_sem=halo_recv.at[1],
        device_id={"space": tile - 1})

    @pl.when(has_down)
    def _():
        to_down.start()

    @pl.when(has_up)
    def _():
        to_up.start()

    offset = (lax.broadcasted_iota(jnp.int32, (cols, cols), 0)
              - lax.broadcasted_iota(jnp.int32, (cols, cols), 1))
    far = offset.astype(jnp.float32)
    band = jnp.where(jnp.abs(offset) <= RADIUS,
                     jnp.exp(-far * far / (2.0 * sigma_cells**2)) / total, 0.0)

    def across(start, size):
        flat = chan[:, :, start : start + size, :].reshape(2 * frames * size, cols)
        out = jnp.dot(flat, band, precision=lax.Precision.HIGHEST,
                      preferred_element_type=jnp.float32)
        horiz[:, :, start : start + size, :] = out.reshape(2, frames, size, cols)

    def corner(j):
        pair, edge = j // 2, j % 2
        side = pair // halves
        group = edge * side * (groups - 1) + (1 - edge) * (1 + side)
        return (pl.multiple_of(group * SUB, SUB),
                pl.multiple_of((pair % halves) * LANES, LANES))

    def down_chunk(j):
        row0, col0 = corner(j)
        window[...] = horiz[:, :, pl.ds(row0, 3 * SUB), pl.ds(col0, LANES)]

        def at(s):
            first = SUB - RADIUS + s
            return window[:, :, first : first + SUB, :]

        out = weights[RADIUS] * at(RADIUS)
        for s in range(RADIUS):
            out = out + weights[s] * (at(s) + at(2 * RADIUS - s))
        return out

    def go_copy(j):
        return pltpu.make_async_remote_copy(
            src_ref=send.at[j], dst_ref=recv.at[me], send_sem=go_send.at[j],
            recv_sem=go_recv.at[me], device_id={"tm": j * stride})

    def scatter(edge):
        def step(k, carry):
            pairs = chunks // 2
            j = 2 * ((mine // 2 + k * (1 + 2 * (mine % 2))) % pairs) + edge
            send[j] = down_chunk(j)

            @pl.when(j * stride != me)
            def _():
                go_copy(j).start()

            @pl.when(j * stride == me)
            def _():
                recv[me] = send[j]

            return carry

        lax.fori_loop(1, chunks // 2 + 1, step, 0)

    across(SUB, rows)
    scatter(0)

    @pl.when(has_up)
    def _():
        to_down.wait_recv()

    @pl.when(has_down)
    def _():
        to_up.wait_recv()

    across(0, SUB)
    across(SUB + rows, SUB)
    scatter(1)

    def back_copy(i):
        return pltpu.make_async_remote_copy(
            src_ref=back.at[i], dst_ref=landed.at[mine], send_sem=ret_send.at[i],
            recv_sem=ret_recv.at[mine], device_id={"tm": i})

    def smooth():
        def forward(i, state):
            @pl.when(i != me)
            def _():
                pltpu.make_async_remote_copy(
                    src_ref=send.at[0], dst_ref=recv.at[i], send_sem=go_send.at[0],
                    recv_sem=go_recv.at[i], device_id={"tm": i}).wait_recv()

            m0, m1, p00, p01, p11 = state
            for f in range(frames):
                num, den = recv[i, 0, f], recv[i, 1, f]
                inv = 1.0 / (1.0 + p00 * den)
                w = den * inv
                e = (num - den * m0) * inv
                k1 = p01 * w
                m0, m1 = m0 + p00 * e, m1 + p01 * e
                p11 = p11 - k1 * p01
                p00, p01 = p00 * inv, p01 * inv
                for slot, value in enumerate((inv, w, e, k1, m0, p00, p01)):
                    saved[i, f, slot] = value
                m0, m1 = ta * m0 + tb * m1, tc * m0 + td * m1
                p00, p01, p11 = (
                    (ta * ta) * p00 + (2.0 * ta * tb) * p01 + ((tb * tb) * p11 + q00),
                    (ta * tc) * p00 + (ta * td + tb * tc) * p01 + ((tb * td) * p11 + q01),
                    (tc * tc) * p00 + (2.0 * tc * td) * p01 + ((td * td) * p11 + q11),
                )
            return m0, m1, p00, p01, p11

        zero = jnp.zeros((SUB, LANES), jnp.float32)
        lax.fori_loop(0, tm_count, forward, (zero, zero, zero + prior0, zero, zero + prior1))

        def backward(n, state):
            i = tm_count - 1 - n
            u0, u1, n00, n01, n11 = state
            for f in reversed(range(frames)):
                inv, w, e, k1, m0, p00, p01 = (saved[i, f, slot] for slot in range(SAVED))
                mean = m0 + p00 * u0 + p01 * u1
                back[i, 0, f] = 1.0 / (1.0 + jnp.exp(-mean))
                back[i, 1, f] = p00 - (
                    p00 * p00 * n00 + 2.0 * (p00 * p01) * n01 + p01 * p01 * n11)
                r0 = e + inv * u0 - k1 * u1
                l00 = w + (inv * inv) * n00 - (2.0 * inv * k1) * n01 + (k1 * k1) * n11
                l01 = inv * n01 - k1 * n11
                u0, u1 = ta * r0 + tc * u1, tb * r0 + td * u1
                n00, n01, n11 = (
                    (ta * ta) * l00 + ((2.0 * ta * tc) * l01 + (tc * tc) * n11),
                    (ta * tb) * l00 + ((ta * td + tb * tc) * l01 + (tc * td) * n11),
                    (tb * tb) * l00 + ((2.0 * tb * td) * l01 + (td * td) * n11),
                )

            return u0, u1, n00, n01, n11

        lax.fori_loop(0, tm_count, backward, (zero,) * 5)

        def give(k, carry):
            back_copy((me + k) % tm_count).start()
            return carry

        lax.fori_loop(1, tm_count, give, 0)
        landed[mine] = back[me]

    if stride == 1:
        smooth()
    else:
        pl.when(me % stride == 0)(smooth)

    def place(k, carry):
        j = (mine + k) % chunks

        @pl.when(j * stride != me)
        def _():
            pltpu.make_async_remote_copy(
                src_ref=back.at[0], dst_ref=landed.at[j], send_sem=ret_send.at[0],
                recv_sem=ret_recv.at[j], device_id={"tm": j * stride}).wait_recv()

        row0, col0 = corner(j)
        occ[:, pl.ds(row0, SUB), pl.ds(col0, LANES)] = landed[j, 0]
        spr[:, pl.ds(row0, SUB), pl.ds(col0, LANES)] = landed[j, 1]
        return carry

    lax.fori_loop(0, chunks, place, 0)

    @pl.when(has_down)
    def _():
        to_down.wait_send()

    @pl.when(has_up)
    def _():
        to_up.wait_send()

    def sent(j, carry):
        @pl.when(j * stride != me)
        def _():
            go_copy(j).wait_send()

        return carry

    lax.fori_loop(0, chunks, sent, 0)

    def returned(i, carry):
        @pl.when(jnp.logical_and(i != me, me % stride == 0))
        def _():
            back_copy(i).wait_send()

        return carry

    lax.fori_loop(0, tm_count, returned, 0)


def solution(mesh):
    tm_count, space_count = mesh.shape["tm"], mesh.shape["space"]

    def body(hits, misses):
        frames, rows, cols = hits.shape
        chunks = (rows // SUB) * (cols // LANES)
        cells = (SUB, LANES)
        vmem = pl.BlockSpec(memory_space=pltpu.VMEM)
        out = jax.ShapeDtypeStruct(hits.shape, jnp.float32)
        return pl.pallas_call(
            functools.partial(kernel, tm_count, space_count),
            out_shape=(out, out),
            in_specs=[pl.BlockSpec(memory_space=pltpu.HBM)] * 2,
            out_specs=(vmem, vmem),
            scratch_shapes=[
                pltpu.VMEM(hits.shape, jnp.int32),
                pltpu.VMEM(hits.shape, jnp.int32),
                pltpu.VMEM((2, frames, rows + 2 * SUB, cols), jnp.float32),
                pltpu.VMEM((2, frames, rows + 2 * SUB, cols), jnp.float32),
                pltpu.VMEM((2, frames, 3 * SUB, LANES), jnp.float32),
                pltpu.VMEM((chunks, 2, frames) + cells, jnp.float32),
                pltpu.VMEM((tm_count, 2, frames) + cells, jnp.float32),
                pltpu.VMEM((tm_count, frames, SAVED) + cells, jnp.float32),
                pltpu.VMEM((tm_count, 2, frames) + cells, jnp.float32),
                pltpu.VMEM((chunks, 2, frames) + cells, jnp.float32),
                pltpu.SemaphoreType.DMA((2,)),
                pltpu.SemaphoreType.DMA((2,)),
                pltpu.SemaphoreType.DMA((chunks,)),
                pltpu.SemaphoreType.DMA((tm_count,)),
                pltpu.SemaphoreType.DMA((tm_count,)),
                pltpu.SemaphoreType.DMA((chunks,)),
                pltpu.SemaphoreType.DMA((2,)),
            ],
            compiler_params=pltpu.CompilerParams(
                collective_id=0, has_side_effects=True, vmem_limit_bytes=48 * 1024 * 1024),
        )(hits, misses)

    placed = P("tm", "space", None)
    return jax.shard_map(body, mesh=mesh, in_specs=(placed, placed),
                         out_specs=(placed, placed), check_vma=False)
```

```python
import functools
import math

import jax
import jax.numpy as jnp
from jax import lax
from jax.experimental import pallas as pl
from jax.experimental.pallas import tpu as pltpu
from jax.sharding import PartitionSpec as P

RADIUS = 7
SCALE_T = 64
SUB = 8
LANES = 128
SAVED = 7

sigma_cells = 3.0
prior_var = 4.0


def dynamics():
    rate = math.sqrt(3.0) / SCALE_T
    factor = math.exp(-rate)
    a, b, c, d = (
        factor * (1.0 + rate),
        factor,
        -factor * rate * rate,
        factor * (1.0 - rate),
    )
    p0, p1 = prior_var, prior_var * rate * rate
    noise = (
        p0 - (a * a * p0 + b * b * p1),
        -(a * c * p0 + b * d * p1),
        p1 - (c * c * p0 + d * d * p1),
    )
    return (a, b, c, d), (p0, p1), noise


def taps():
    raw = [math.exp(-o * o / (2.0 * sigma_cells**2)) for o in range(-RADIUS, RADIUS + 1)]
    total = sum(raw)
    return [r / total for r in raw], total


def corner(j, groups, halves):
    pair, edge = j // 2, j % 2
    side = pair // halves
    group = edge * side * (groups - 1) + (1 - edge) * (1 + side)
    return group * SUB, (pair % halves) * LANES


def spread_out(landed, occ, spr, sems):
    groups, halves = occ.shape[1] // SUB, occ.shape[2] // LANES
    copies = []
    for j in range(groups * halves):
        row0, col0 = corner(j, groups, halves)
        for k, out in enumerate((occ, spr)):
            copies.append(pltpu.make_async_copy(
                landed.at[j, k], out.at[:, row0 : row0 + SUB, col0 : col0 + LANES],
                sems.at[j, k]))
    for copy in copies:
        copy.start()
    for copy in copies:
        copy.wait()


def kernel(tm_count, space_count, hits_hbm, misses_hbm, landed, hits, misses, chan, horiz,
           window, send, recv, saved, back, halo_send, halo_recv, go_send, go_recv, ret_send, ret_recv, load):
    load_hits = pltpu.make_async_copy(hits_hbm, hits, load.at[0])
    load_misses = pltpu.make_async_copy(misses_hbm, misses, load.at[1])
    load_hits.start()
    load_misses.start()
    frames, rows, cols = hits.shape
    groups = rows // SUB
    halves = cols // LANES
    chunks = (rows // SUB) * halves
    stride = tm_count // chunks
    me = lax.axis_index("tm")
    tile = lax.axis_index("space")
    mine = me // stride
    (ta, tb, tc, td), (prior0, prior1), (q00, q01, q11) = dynamics()
    weights, total = taps()
    has_up = tile > 0
    has_down = tile < space_count - 1
    barrier = pltpu.get_barrier_semaphore()

    def greet(k, carry):
        pl.semaphore_signal(barrier, inc=1, device_id={"tm": (me + k) % tm_count})
        return carry

    lax.fori_loop(1, tm_count, greet, 0)

    @pl.when(has_up)
    def _():
        pl.semaphore_signal(barrier, inc=1, device_id={"space": tile - 1})

    @pl.when(has_down)
    def _():
        pl.semaphore_signal(barrier, inc=1, device_id={"space": tile + 1})

    own = pl.ds(SUB, rows)
    load_hits.wait()
    load_misses.wait()

    def observe(f, carry):
        h, m = hits[f], misses[f]
        hp = h.astype(jnp.float32) + 1.0
        mp = m.astype(jnp.float32) + 1.0
        both = hp + mp
        weight = (h + m).astype(jnp.float32) * hp * mp / (both * both)
        chan[0, f, own, :] = weight * jnp.log(hp / mp)
        chan[1, f, own, :] = weight
        return carry

    lax.fori_loop(0, frames, observe, 0)

    @pl.when(jnp.logical_not(has_up))
    def _():
        chan[:, :, 0:SUB, :] = jnp.zeros((2, frames, SUB, cols), jnp.float32)

    @pl.when(jnp.logical_not(has_down))
    def _():
        chan[:, :, SUB + rows :, :] = jnp.zeros((2, frames, SUB, cols), jnp.float32)

    neighbours = has_up.astype(jnp.int32) + has_down.astype(jnp.int32)
    pl.semaphore_wait(barrier, tm_count - 1 + neighbours)

    to_down = pltpu.make_async_remote_copy(
        src_ref=chan.at[:, :, pl.ds(rows, SUB), :],
        dst_ref=chan.at[:, :, pl.ds(0, SUB), :],
        send_sem=halo_send.at[0], recv_sem=halo_recv.at[0],
        device_id={"space": tile + 1})
    to_up = pltpu.make_async_remote_copy(
        src_ref=chan.at[:, :, pl.ds(SUB, SUB), :],
        dst_ref=chan.at[:, :, pl.ds(SUB + rows, SUB), :],
        send_sem=halo_send.at[1], recv_sem=halo_recv.at[1],
        device_id={"space": tile - 1})

    @pl.when(has_down)
    def _():
        to_down.start()

    @pl.when(has_up)
    def _():
        to_up.start()

    offset = (lax.broadcasted_iota(jnp.int32, (cols, cols), 0)
              - lax.broadcasted_iota(jnp.int32, (cols, cols), 1))
    far = offset.astype(jnp.float32)
    band = jnp.where(jnp.abs(offset) <= RADIUS,
                     jnp.exp(-far * far / (2.0 * sigma_cells**2)) / total, 0.0)

    band_high = band.astype(jnp.bfloat16)
    band_low = (band - band_high.astype(jnp.float32)).astype(jnp.bfloat16)

    def across(start, size):
        flat = chan[:, :, start : start + size, :].reshape(2 * frames * size, cols)
        high = flat.astype(jnp.bfloat16)
        low = (flat - high.astype(jnp.float32)).astype(jnp.bfloat16)
        dot = functools.partial(jnp.dot, preferred_element_type=jnp.float32)
        out = dot(high, band_high) + (dot(low, band_high) + dot(high, band_low))
        horiz[:, :, start : start + size, :] = out.reshape(2, frames, size, cols)

    def down_chunk(j):
        row0, col0 = corner(j, groups, halves)
        row0, col0 = pl.multiple_of(row0, SUB), pl.multiple_of(col0, LANES)
        window[...] = horiz[:, :, pl.ds(row0, 3 * SUB), pl.ds(col0, LANES)]

        def at(s):
            first = SUB - RADIUS + s
            return window[:, :, first : first + SUB, :]

        out = weights[RADIUS] * at(RADIUS)
        for s in range(RADIUS):
            out = out + weights[s] * (at(s) + at(2 * RADIUS - s))
        return out

    def go_copy(j):
        return pltpu.make_async_remote_copy(
            src_ref=send.at[j], dst_ref=recv.at[me], send_sem=go_send.at[j],
            recv_sem=go_recv.at[me], device_id={"tm": j * stride})

    def scatter(edge):
        def step(k, carry):
            pairs = chunks // 2
            j = 2 * ((mine // 2 + k * (1 + 2 * (mine % 2))) % pairs) + edge
            send[j] = down_chunk(j)

            @pl.when(j * stride != me)
            def _():
                go_copy(j).start()

            @pl.when(j * stride == me)
            def _():
                recv[me] = send[j]

            return carry

        lax.fori_loop(1, chunks // 2 + 1, step, 0)

    across(SUB, rows)
    scatter(0)

    @pl.when(has_up)
    def _():
        to_down.wait_recv()

    @pl.when(has_down)
    def _():
        to_up.wait_recv()

    across(0, SUB)
    across(SUB + rows, SUB)
    scatter(1)

    def back_copy(i):
        return pltpu.make_async_remote_copy(
            src_ref=back.at[i], dst_ref=landed.at[mine], send_sem=ret_send.at[i],
            recv_sem=ret_recv.at[mine], device_id={"tm": i})

    def smooth():
        def forward(i, state):
            @pl.when(i != me)
            def _():
                pltpu.make_async_remote_copy(
                    src_ref=send.at[0], dst_ref=recv.at[i], send_sem=go_send.at[0],
                    recv_sem=go_recv.at[i], device_id={"tm": i}).wait_recv()

            m0, m1, p00, p01, p11 = state
            for f in range(frames):
                num, den = recv[i, 0, f], recv[i, 1, f]
                inv = 1.0 / (1.0 + p00 * den)
                w = den * inv
                e = (num - den * m0) * inv
                k1 = p01 * w
                m0, m1 = m0 + p00 * e, m1 + p01 * e
                p11 = p11 - k1 * p01
                p00, p01 = p00 * inv, p01 * inv
                for slot, value in enumerate((inv, w, e, k1, m0, p00, p01)):
                    saved[i, f, slot] = value
                m0, m1 = ta * m0 + tb * m1, tc * m0 + td * m1
                p00, p01, p11 = (
                    (ta * ta) * p00 + (2.0 * ta * tb) * p01 + ((tb * tb) * p11 + q00),
                    (ta * tc) * p00 + (ta * td + tb * tc) * p01 + ((tb * td) * p11 + q01),
                    (tc * tc) * p00 + (2.0 * tc * td) * p01 + ((td * td) * p11 + q11),
                )
            return m0, m1, p00, p01, p11

        zero = jnp.zeros((SUB, LANES), jnp.float32)
        lax.fori_loop(0, tm_count, forward, (zero, zero, zero + prior0, zero, zero + prior1))

        def backward(n, state):
            i = tm_count - 1 - n
            u0, u1, n00, n01, n11 = state
            for f in reversed(range(frames)):
                inv, w, e, k1, m0, p00, p01 = (saved[i, f, slot] for slot in range(SAVED))
                mean = m0 + p00 * u0 + p01 * u1
                back[i, 0, f] = 1.0 / (1.0 + jnp.exp(-mean))
                back[i, 1, f] = p00 - (
                    p00 * p00 * n00 + 2.0 * (p00 * p01) * n01 + p01 * p01 * n11)
                r0 = e + inv * u0 - k1 * u1
                l00 = w + (inv * inv) * n00 - (2.0 * inv * k1) * n01 + (k1 * k1) * n11
                l01 = inv * n01 - k1 * n11
                u0, u1 = ta * r0 + tc * u1, tb * r0 + td * u1
                n00, n01, n11 = (
                    (ta * ta) * l00 + ((2.0 * ta * tc) * l01 + (tc * tc) * n11),
                    (ta * tb) * l00 + ((ta * td + tb * tc) * l01 + (tc * td) * n11),
                    (tb * tb) * l00 + ((2.0 * tb * td) * l01 + (td * td) * n11),
                )

            return u0, u1, n00, n01, n11

        lax.fori_loop(0, tm_count, backward, (zero,) * 5)

        def give(k, carry):
            back_copy((me + k) % tm_count).start()
            return carry

        lax.fori_loop(1, tm_count, give, 0)
        landed[mine] = back[me]

    if stride == 1:
        smooth()
    else:
        pl.when(me % stride == 0)(smooth)

    def place(k, carry):
        j = (mine + k) % chunks

        @pl.when(j * stride != me)
        def _():
            pltpu.make_async_remote_copy(
                src_ref=back.at[0], dst_ref=landed.at[j], send_sem=ret_send.at[0],
                recv_sem=ret_recv.at[j], device_id={"tm": j * stride}).wait_recv()

        return carry

    lax.fori_loop(0, chunks, place, 0)

    @pl.when(has_down)
    def _():
        to_down.wait_send()

    @pl.when(has_up)
    def _():
        to_up.wait_send()

    def sent(j, carry):
        @pl.when(j * stride != me)
        def _():
            go_copy(j).wait_send()

        return carry

    lax.fori_loop(0, chunks, sent, 0)

    def returned(i, carry):
        @pl.when(jnp.logical_and(i != me, me % stride == 0))
        def _():
            back_copy(i).wait_send()

        return carry

    lax.fori_loop(0, tm_count, returned, 0)


def solution(mesh):
    tm_count, space_count = mesh.shape["tm"], mesh.shape["space"]

    def body(hits, misses):
        frames, rows, cols = hits.shape
        chunks = (rows // SUB) * (cols // LANES)
        cells = (SUB, LANES)
        vmem = pl.BlockSpec(memory_space=pltpu.VMEM)
        out = jax.ShapeDtypeStruct(hits.shape, jnp.float32)
        landed = pl.pallas_call(
            functools.partial(kernel, tm_count, space_count),
            out_shape=jax.ShapeDtypeStruct((chunks, 2, frames) + cells, jnp.float32),
            in_specs=[pl.BlockSpec(memory_space=pltpu.HBM)] * 2,
            out_specs=vmem,
            scratch_shapes=[
                pltpu.VMEM(hits.shape, jnp.int32),
                pltpu.VMEM(hits.shape, jnp.int32),
                pltpu.VMEM((2, frames, rows + 2 * SUB, cols), jnp.float32),
                pltpu.VMEM((2, frames, rows + 2 * SUB, cols), jnp.float32),
                pltpu.VMEM((2, frames, 3 * SUB, LANES), jnp.float32),
                pltpu.VMEM((chunks, 2, frames) + cells, jnp.float32),
                pltpu.VMEM((tm_count, 2, frames) + cells, jnp.float32),
                pltpu.VMEM((tm_count, frames, SAVED) + cells, jnp.float32),
                pltpu.VMEM((tm_count, 2, frames) + cells, jnp.float32),
                pltpu.SemaphoreType.DMA((2,)),
                pltpu.SemaphoreType.DMA((2,)),
                pltpu.SemaphoreType.DMA((chunks,)),
                pltpu.SemaphoreType.DMA((tm_count,)),
                pltpu.SemaphoreType.DMA((tm_count,)),
                pltpu.SemaphoreType.DMA((chunks,)),
                pltpu.SemaphoreType.DMA((2,)),
            ],
            compiler_params=pltpu.CompilerParams(
                collective_id=0, has_side_effects=True, vmem_limit_bytes=48 * 1024 * 1024),
        )(hits, misses)
        hbm = pl.BlockSpec(memory_space=pltpu.HBM)
        return pl.pallas_call(
            spread_out,
            out_shape=(out, out),
            in_specs=[vmem],
            out_specs=(hbm, hbm),
            scratch_shapes=[pltpu.SemaphoreType.DMA((chunks, 2))],
            compiler_params=pltpu.CompilerParams(vmem_limit_bytes=8 * 1024 * 1024),
        )(landed)

    placed = P("tm", "space", None)
    return jax.shard_map(body, mesh=mesh, in_specs=(placed, placed),
                         out_specs=(placed, placed), check_vma=False)
```

```python
import functools
import math

import jax
import jax.numpy as jnp
from jax import lax
from jax.experimental import pallas as pl
from jax.experimental.pallas import tpu as pltpu
from jax.sharding import PartitionSpec as P

RADIUS = 7
SCALE_T = 64
SUB = 8
LANES = 128
SAVED = 7

sigma_cells = 3.0
prior_var = 4.0


def dynamics():
    rate = math.sqrt(3.0) / SCALE_T
    factor = math.exp(-rate)
    a, b, c, d = (
        factor * (1.0 + rate),
        factor,
        -factor * rate * rate,
        factor * (1.0 - rate),
    )
    p0, p1 = prior_var, prior_var * rate * rate
    noise = (
        p0 - (a * a * p0 + b * b * p1),
        -(a * c * p0 + b * d * p1),
        p1 - (c * c * p0 + d * d * p1),
    )
    return (a, b, c, d), (p0, p1), noise


def taps():
    raw = [math.exp(-o * o / (2.0 * sigma_cells**2)) for o in range(-RADIUS, RADIUS + 1)]
    total = sum(raw)
    return [r / total for r in raw], total


def corner(j, groups, halves):
    pair, edge = j // 2, j % 2
    side = pair // halves
    group = edge * side * (groups - 1) + (1 - edge) * (1 + side)
    return group * SUB, (pair % halves) * LANES


def spread_out(landed, occ, spr, sems):
    groups, halves = occ.shape[1] // SUB, occ.shape[2] // LANES
    copies = []
    for j in range(groups * halves):
        row0, col0 = corner(j, groups, halves)
        for k, out in enumerate((occ, spr)):
            copies.append(pltpu.make_async_copy(
                landed.at[j, k], out.at[:, row0 : row0 + SUB, col0 : col0 + LANES],
                sems.at[j, k]))
    for copy in copies:
        copy.start()
    for copy in copies:
        copy.wait()


def kernel(tm_count, space_count, hits_hbm, misses_hbm, landed, hits, misses, chan, horiz,
           window, send, recv, saved, back, halo_send, halo_recv, go_send, go_recv, ret_send, ret_recv, load):
    load_hits = pltpu.make_async_copy(hits_hbm, hits, load.at[0])
    load_misses = pltpu.make_async_copy(misses_hbm, misses, load.at[1])
    load_hits.start()
    load_misses.start()
    frames, rows, cols = hits.shape
    groups = rows // SUB
    halves = cols // LANES
    chunks = (rows // SUB) * halves
    stride = tm_count // chunks
    me = lax.axis_index("tm")
    tile = lax.axis_index("space")
    mine = me // stride
    (ta, tb, tc, td), (prior0, prior1), (q00, q01, q11) = dynamics()
    weights, total = taps()
    has_up = tile > 0
    has_down = tile < space_count - 1
    barrier = pltpu.get_barrier_semaphore()

    def greet(k, carry):
        pl.semaphore_signal(barrier, inc=1, device_id={"tm": (me + k) % tm_count})
        return carry

    lax.fori_loop(1, tm_count, greet, 0)

    @pl.when(has_up)
    def _():
        pl.semaphore_signal(barrier, inc=1, device_id={"space": tile - 1})

    @pl.when(has_down)
    def _():
        pl.semaphore_signal(barrier, inc=1, device_id={"space": tile + 1})

    own = pl.ds(SUB, rows)
    load_hits.wait()
    load_misses.wait()

    def observe(f, carry):
        h, m = hits[f], misses[f]
        hp = h.astype(jnp.float32) + 1.0
        mp = m.astype(jnp.float32) + 1.0
        both = hp + mp
        weight = (h + m).astype(jnp.float32) * hp * mp / (both * both)
        chan[0, f, own, :] = weight * jnp.log(hp / mp)
        chan[1, f, own, :] = weight
        return carry

    lax.fori_loop(0, frames, observe, 0)

    @pl.when(jnp.logical_not(has_up))
    def _():
        chan[:, :, 0:SUB, :] = jnp.zeros((2, frames, SUB, cols), jnp.float32)

    @pl.when(jnp.logical_not(has_down))
    def _():
        chan[:, :, SUB + rows :, :] = jnp.zeros((2, frames, SUB, cols), jnp.float32)

    neighbours = has_up.astype(jnp.int32) + has_down.astype(jnp.int32)
    pl.semaphore_wait(barrier, tm_count - 1 + neighbours)

    to_down = pltpu.make_async_remote_copy(
        src_ref=chan.at[:, :, pl.ds(rows, SUB), :],
        dst_ref=chan.at[:, :, pl.ds(0, SUB), :],
        send_sem=halo_send.at[0], recv_sem=halo_recv.at[0],
        device_id={"space": tile + 1})
    to_up = pltpu.make_async_remote_copy(
        src_ref=chan.at[:, :, pl.ds(SUB, SUB), :],
        dst_ref=chan.at[:, :, pl.ds(SUB + rows, SUB), :],
        send_sem=halo_send.at[1], recv_sem=halo_recv.at[1],
        device_id={"space": tile - 1})

    @pl.when(has_down)
    def _():
        to_down.start()

    @pl.when(has_up)
    def _():
        to_up.start()

    offset = (lax.broadcasted_iota(jnp.int32, (cols, cols), 0)
              - lax.broadcasted_iota(jnp.int32, (cols, cols), 1))
    far = offset.astype(jnp.float32)
    band = jnp.where(jnp.abs(offset) <= RADIUS,
                     jnp.exp(-far * far / (2.0 * sigma_cells**2)) / total, 0.0)

    band_high = band.astype(jnp.bfloat16)
    band_low = (band - band_high.astype(jnp.float32)).astype(jnp.bfloat16)

    def across(start, size):
        flat = chan[:, :, start : start + size, :].reshape(2 * frames * size, cols)
        high = flat.astype(jnp.bfloat16)
        low = (flat - high.astype(jnp.float32)).astype(jnp.bfloat16)
        dot = functools.partial(jnp.dot, preferred_element_type=jnp.float32)
        out = dot(high, band_high) + (dot(low, band_high) + dot(high, band_low))
        horiz[:, :, start : start + size, :] = out.reshape(2, frames, size, cols)

    def down_chunk(j):
        row0, col0 = corner(j, groups, halves)
        row0, col0 = pl.multiple_of(row0, SUB), pl.multiple_of(col0, LANES)
        window[...] = horiz[:, :, pl.ds(row0, 3 * SUB), pl.ds(col0, LANES)]

        def at(s):
            first = SUB - RADIUS + s
            return window[:, :, first : first + SUB, :]

        out = weights[RADIUS] * at(RADIUS)
        for s in range(RADIUS):
            out = out + weights[s] * (at(s) + at(2 * RADIUS - s))
        return out

    def go_copy(j):
        return pltpu.make_async_remote_copy(
            src_ref=send.at[j], dst_ref=recv.at[me], send_sem=go_send.at[j],
            recv_sem=go_recv.at[me], device_id={"tm": j * stride})

    def scatter(edge):
        def step(k, carry):
            pairs = chunks // 2
            j = 2 * ((mine // 2 + k) % pairs) + edge
            send[j] = down_chunk(j)

            @pl.when(j * stride != me)
            def _():
                go_copy(j).start()

            @pl.when(j * stride == me)
            def _():
                recv[me] = send[j]

            return carry

        lax.fori_loop(1, chunks // 2 + 1, step, 0)

    across(SUB, rows)
    scatter(0)

    @pl.when(has_up)
    def _():
        to_down.wait_recv()

    @pl.when(has_down)
    def _():
        to_up.wait_recv()

    across(0, SUB)
    across(SUB + rows, SUB)
    scatter(1)

    def back_copy(i):
        return pltpu.make_async_remote_copy(
            src_ref=back.at[i], dst_ref=landed.at[mine], send_sem=ret_send.at[i],
            recv_sem=ret_recv.at[mine], device_id={"tm": i})

    def smooth():
        def forward(i, state):
            @pl.when(i != me)
            def _():
                pltpu.make_async_remote_copy(
                    src_ref=send.at[0], dst_ref=recv.at[i], send_sem=go_send.at[0],
                    recv_sem=go_recv.at[i], device_id={"tm": i}).wait_recv()

            m0, m1, p00, p01, p11 = state
            for f in range(frames):
                num, den = recv[i, 0, f], recv[i, 1, f]
                inv = 1.0 / (1.0 + p00 * den)
                w = den * inv
                e = (num - den * m0) * inv
                k1 = p01 * w
                m0, m1 = m0 + p00 * e, m1 + p01 * e
                p11 = p11 - k1 * p01
                p00, p01 = p00 * inv, p01 * inv
                for slot, value in enumerate((inv, w, e, k1, m0, p00, p01)):
                    saved[i, f, slot] = value
                m0, m1 = ta * m0 + tb * m1, tc * m0 + td * m1
                p00, p01, p11 = (
                    (ta * ta) * p00 + (2.0 * ta * tb) * p01 + ((tb * tb) * p11 + q00),
                    (ta * tc) * p00 + (ta * td + tb * tc) * p01 + ((tb * td) * p11 + q01),
                    (tc * tc) * p00 + (2.0 * tc * td) * p01 + ((td * td) * p11 + q11),
                )
            return m0, m1, p00, p01, p11

        zero = jnp.zeros((SUB, LANES), jnp.float32)
        lax.fori_loop(0, tm_count, forward, (zero, zero, zero + prior0, zero, zero + prior1))

        def backward(n, state):
            i = tm_count - 1 - n
            u0, u1, n00, n01, n11 = state
            for f in reversed(range(frames)):
                inv, w, e, k1, m0, p00, p01 = (saved[i, f, slot] for slot in range(SAVED))
                mean = m0 + p00 * u0 + p01 * u1
                back[i, 0, f] = 1.0 / (1.0 + jnp.exp(-mean))
                back[i, 1, f] = p00 - (
                    p00 * p00 * n00 + 2.0 * (p00 * p01) * n01 + p01 * p01 * n11)
                r0 = e + inv * u0 - k1 * u1
                l00 = w + (inv * inv) * n00 - (2.0 * inv * k1) * n01 + (k1 * k1) * n11
                l01 = inv * n01 - k1 * n11
                u0, u1 = ta * r0 + tc * u1, tb * r0 + td * u1
                n00, n01, n11 = (
                    (ta * ta) * l00 + ((2.0 * ta * tc) * l01 + (tc * tc) * n11),
                    (ta * tb) * l00 + ((ta * td + tb * tc) * l01 + (tc * td) * n11),
                    (tb * tb) * l00 + ((2.0 * tb * td) * l01 + (td * td) * n11),
                )

            return u0, u1, n00, n01, n11

        lax.fori_loop(0, tm_count, backward, (zero,) * 5)

        def give(k, carry):
            back_copy((me + k) % tm_count).start()
            return carry

        lax.fori_loop(1, tm_count, give, 0)
        landed[mine] = back[me]

    if stride == 1:
        smooth()
    else:
        pl.when(me % stride == 0)(smooth)

    def place(k, carry):
        j = (mine + k) % chunks

        @pl.when(j * stride != me)
        def _():
            pltpu.make_async_remote_copy(
                src_ref=back.at[0], dst_ref=landed.at[j], send_sem=ret_send.at[0],
                recv_sem=ret_recv.at[j], device_id={"tm": j * stride}).wait_recv()

        return carry

    lax.fori_loop(0, chunks, place, 0)

    @pl.when(has_down)
    def _():
        to_down.wait_send()

    @pl.when(has_up)
    def _():
        to_up.wait_send()

    def sent(j, carry):
        @pl.when(j * stride != me)
        def _():
            go_copy(j).wait_send()

        return carry

    lax.fori_loop(0, chunks, sent, 0)

    def returned(i, carry):
        @pl.when(jnp.logical_and(i != me, me % stride == 0))
        def _():
            back_copy(i).wait_send()

        return carry

    lax.fori_loop(0, tm_count, returned, 0)


def solution(mesh):
    tm_count, space_count = mesh.shape["tm"], mesh.shape["space"]

    def body(hits, misses):
        frames, rows, cols = hits.shape
        chunks = (rows // SUB) * (cols // LANES)
        cells = (SUB, LANES)
        vmem = pl.BlockSpec(memory_space=pltpu.VMEM)
        out = jax.ShapeDtypeStruct(hits.shape, jnp.float32)
        landed = pl.pallas_call(
            functools.partial(kernel, tm_count, space_count),
            out_shape=jax.ShapeDtypeStruct((chunks, 2, frames) + cells, jnp.float32),
            in_specs=[pl.BlockSpec(memory_space=pltpu.HBM)] * 2,
            out_specs=vmem,
            scratch_shapes=[
                pltpu.VMEM(hits.shape, jnp.int32),
                pltpu.VMEM(hits.shape, jnp.int32),
                pltpu.VMEM((2, frames, rows + 2 * SUB, cols), jnp.float32),
                pltpu.VMEM((2, frames, rows + 2 * SUB, cols), jnp.float32),
                pltpu.VMEM((2, frames, 3 * SUB, LANES), jnp.float32),
                pltpu.VMEM((chunks, 2, frames) + cells, jnp.float32),
                pltpu.VMEM((tm_count, 2, frames) + cells, jnp.float32),
                pltpu.VMEM((tm_count, frames, SAVED) + cells, jnp.float32),
                pltpu.VMEM((tm_count, 2, frames) + cells, jnp.float32),
                pltpu.SemaphoreType.DMA((2,)),
                pltpu.SemaphoreType.DMA((2,)),
                pltpu.SemaphoreType.DMA((chunks,)),
                pltpu.SemaphoreType.DMA((tm_count,)),
                pltpu.SemaphoreType.DMA((tm_count,)),
                pltpu.SemaphoreType.DMA((chunks,)),
                pltpu.SemaphoreType.DMA((2,)),
            ],
            compiler_params=pltpu.CompilerParams(
                collective_id=0, has_side_effects=True, vmem_limit_bytes=48 * 1024 * 1024),
        )(hits, misses)
        hbm = pl.BlockSpec(memory_space=pltpu.HBM)
        return pl.pallas_call(
            spread_out,
            out_shape=(out, out),
            in_specs=[vmem],
            out_specs=(hbm, hbm),
            scratch_shapes=[pltpu.SemaphoreType.DMA((chunks, 2))],
            compiler_params=pltpu.CompilerParams(vmem_limit_bytes=8 * 1024 * 1024),
        )(landed)

    placed = P("tm", "space", None)
    return jax.shard_map(body, mesh=mesh, in_specs=(placed, placed),
                         out_specs=(placed, placed), check_vma=False)
```
